128 devices in a mesh: pool: 16 (over x_lo, z, core), cp: 8 (over x_hi, y).
Axes of the slice: x: 4 (x_hi: 2, x_lo: 2; x = x_hi * 2 + x_lo), y: 4, z: 4, core: 2. Of those that a mesh axis runs over, the one named last changes fastest.
Arguments:
- queries: bfloat16 [16, 1024, 4096], P('pool', 'cp'), may hold values from -15 to 15
- span_keys: bfloat16 [16, 1024, 512], P('pool', 'cp'), may hold values from -6 to 6
- span_values: bfloat16 [16, 1024, 512], P('pool', 'cp'), may hold values from -6 to 6
- pool_keys: bfloat16 [384, 128, 512], P('pool'), may hold values from -6 to 6
- pool_values: bfloat16 [384, 128, 512], P('pool'), may hold values from -6 to 6
- page_ids: int32 [16, 32], replicated, may hold values from 0 to 383, as said below
- prefix_pages: int32 [16], replicated, may hold values from 1 to 32, as said below
Outputs:
- attended: float32 [16, 1024, 4096], P('pool', 'cp')
The draws below stay inside these ranges and needn't reach their ends.
Inputs may be any that keep to these rules, and one draw needn't show every extreme that they name: `page_ids`: page p is held by index p // 24 of pool. Among the first prefix_pages[r] entries of a request, one owner holds at most 2 pages, all different; entries beyond that are unused. `prefix_pages`: some request has all 32 entries in use.
All inputs are finite; a program needn't handle non-finite values.
Results may differ from the reference program's by a relative error of at most 0.002.
Values may be sent and summed in bfloat16 or wider, within the bound.
A program may use at most 128 MiB of HBM per device.

```python
import jax
import jax.numpy as jnp
from jax import lax

HEAD_DIM = 128
HEADS = 32
KV_HEADS = 4
PAGE = 128
CAP = 2
PAGES_DEV = 24
TOK_DEV = 128
SPAN = 1024
REQS = 16
SLOTS = 32
POOL_PAGES = 384


def draw_queries(key, part):
    shape = (REQS, SPAN, HEADS * HEAD_DIM)
    noise_key = jax.random.fold_in(key, 5)
    return jnp.clip(2.5 * jax.random.normal(noise_key, shape, jnp.float32), -15.0, 15.0).astype(jnp.bfloat16)


def draw_span_keys(key, part):
    shape = (REQS, SPAN, KV_HEADS * HEAD_DIM)
    noise_key = jax.random.fold_in(key, 9)
    return jnp.clip(jax.random.normal(noise_key, shape, jnp.float32), -6.0, 6.0).astype(jnp.bfloat16)


def one_list(key):
    key_perm, key_base, key_off = jax.random.split(key, 3)
    owner_count = SLOTS // CAP
    band = PAGES_DEV // CAP
    perm = jax.random.permutation(key_perm, owner_count)
    slot = jnp.arange(SLOTS)
    owner = perm[slot // CAP]
    base = jax.random.randint(key_base, (owner_count,), 0, PAGES_DEV)[slot // CAP]
    offset = jax.random.randint(key_off, (SLOTS,), 0, band)
    local = (base + slot % CAP * band + offset) % PAGES_DEV
    return (owner * PAGES_DEV + local).astype(jnp.int32)


def draw_page_ids(key, part):
    keys = jax.random.split(jax.random.fold_in(key, 11), REQS)
    return jax.vmap(one_list)(keys)


def draw_prefix_pages(key, part):
    key_len, key_which = jax.random.split(jax.random.fold_in(key, 13))
    lengths = jax.random.randint(key_len, (REQS,), 1, SLOTS + 1)
    which = jax.random.randint(key_which, (), 0, REQS)
    return lengths.at[which].set(SLOTS).astype(jnp.int32)


def block_scale(stream_key, dims, shards, least, high):
    gain, own = 1.0, jax.random.fold_in(stream_key, 6)
    for position, parts in shards:
        steps = jnp.exp(jax.random.uniform(jax.random.fold_in(own, position), (parts,), jnp.float32, least / len(shards), high / len(shards)))
        gain = gain * jnp.repeat(steps, dims[position] // parts).reshape([-1 if axis == position else 1 for axis in range(len(dims))])
    return gain


def centred(stream_key, extent, deviation, most, pieces=(), kind=jnp.bfloat16):
    level = block_scale(stream_key, extent, pieces, -0.22, 0.18) if pieces else 1.0
    values = jax.random.normal(stream_key, extent, jnp.float32) * deviation * level
    return jnp.minimum(jnp.maximum(values, -most), most).astype(kind)


def setup_inputs(seed: int = 0) -> dict:
    arg_keys = jax.random.split(jax.random.key(seed), 8)
    queries = draw_queries(jax.random.fold_in(arg_keys[7], 71), 0)
    span_keys = draw_span_keys(jax.random.fold_in(arg_keys[7], 71), 0)
    span_values = centred(arg_keys[2], (REQS, SPAN, KV_HEADS * HEAD_DIM), 1.0, 6.0, ((0, 16), (1, 8)))
    pool_keys = centred(arg_keys[3], (POOL_PAGES, PAGE, KV_HEADS * HEAD_DIM), 1.0, 6.0, ((0, 16),))
    pool_values = centred(arg_keys[4], (POOL_PAGES, PAGE, KV_HEADS * HEAD_DIM), 1.0, 6.0, ((0, 16),))
    page_ids = draw_page_ids(jax.random.fold_in(arg_keys[7], 71), 0)
    prefix_pages = draw_prefix_pages(jax.random.fold_in(arg_keys[7], 71), 0)
    return dict(queries=queries, span_keys=span_keys, span_values=span_values, pool_keys=pool_keys, pool_values=pool_values, page_ids=page_ids, prefix_pages=prefix_pages)


NEG_FILL = -1e30


def one_request(inputs, pool_keys, pool_values):
    queries, span_keys, span_values, page_list, live_pages = inputs
    groups = HEADS // KV_HEADS
    width = KV_HEADS * HEAD_DIM
    prefix_keys = pool_keys[page_list].reshape(SLOTS * PAGE, width)
    prefix_values = pool_values[page_list].reshape(SLOTS * PAGE, width)
    key_row_set = jnp.concatenate([prefix_keys, span_keys], 0).astype(jnp.float32).reshape(-1, KV_HEADS, HEAD_DIM)
    value_row_set = jnp.concatenate([prefix_values, span_values], 0).astype(jnp.float32).reshape(-1, KV_HEADS, HEAD_DIM)
    slot_live = jnp.repeat(jnp.arange(SLOTS, dtype=jnp.int32) < live_pages, PAGE)
    span_pos = jnp.arange(SPAN, dtype=jnp.int32)
    score_scale = HEAD_DIM ** -0.5

    def block(index):
        begin = (index * TOK_DEV).astype(jnp.int32)
        query_block_rows = lax.dynamic_slice_in_dim(queries, begin, TOK_DEV, 0).astype(jnp.float32)
        query_block_rows = query_block_rows.reshape(TOK_DEV, KV_HEADS, groups, HEAD_DIM)
        query_pos = begin + jnp.arange(TOK_DEV, dtype=jnp.int32)
        visible = jnp.concatenate([jnp.broadcast_to(slot_live[None, :], (TOK_DEV, SLOTS * PAGE)), span_pos[None, :] <= query_pos[:, None]], 1)
        logit_scores = jnp.einsum("swxl,cwl->swxc", query_block_rows, key_row_set) * score_scale
        live = visible[:, None, None, :]
        logit_scores = jnp.where(live, logit_scores, NEG_FILL)
        peak = jnp.max(logit_scores, axis=-1, keepdims=True)
        softmax_weights = jnp.where(live, jnp.exp(logit_scores - peak), 0.0).astype(jnp.bfloat16)
        denom = jnp.sum(softmax_weights.astype(jnp.float32), axis=-1)
        weighted_values = jnp.einsum("unqy,ynx->unqx", softmax_weights.astype(jnp.float32), value_row_set)
        return (weighted_values / denom[..., None]).reshape(TOK_DEV, HEADS * HEAD_DIM)

    outputs = lax.map(block, jnp.arange(SPAN // TOK_DEV, dtype=jnp.int32))
    return outputs.reshape(SPAN, HEADS * HEAD_DIM)


def reference(queries, span_keys, span_values, pool_keys, pool_values, page_ids, prefix_pages):
    def single(inputs):
        return one_request(inputs, pool_keys, pool_values)

    return lax.map(single, (queries, span_keys, span_values, page_ids, prefix_pages))
```

```python
import functools

import jax
import jax.numpy as jnp
import numpy as np
from jax import lax
from jax.experimental import pallas as pl
from jax.experimental.pallas import tpu as pltpu
from jax.sharding import PartitionSpec as P

HEAD_DIM = 128
HEADS = 32
KV_HEADS = 4
PAGES_DEV = 24
SLOTS = 32
TOK = 128
GROUPS = HEADS // KV_HEADS
COLS = GROUPS * HEAD_DIM

ROWS = 512
KEYS = 1024
VROWS = 144
NEG = -1e30
SCALE2 = float(HEAD_DIM**-0.5 * np.log2(np.e))
MESH = pl.DeviceIdType.MESH

CHUNK_OWNERS = ((0, 1, 2, 6), (3, 7, 8, 9), (10, 11, 14, 15), (4, 5, 12, 13))
SEND_ORDER = (1, 2, 6, 8, 3, 7, 9, 10, 14, 11, 15, 4, 12, 5, 13)
BLOCK_XOR = (0, 1, 3, 2)
BF16 = jnp.bfloat16
F32 = jnp.float32


def xor(index, offset):
    for bit in range(4):
        if offset >> bit & 1:
            index = index + (1 << bit) * (1 - 2 * ((index // (1 << bit)) % 2))
    return index


def schedule(u):
    chunk = jnp.where(u < 6, u // 3, jnp.where(u < 8, u - 6, u // 4))
    block = jnp.where(u < 6, u % 3, jnp.where(u < 8, 3, jnp.where(u < 16, u % 4, 3 - u % 4)))
    return chunk, block


def kernel(
    pid, npages, ids_ref, q_ref, sk_ref, sv_ref, pk_ref, pv_ref,
    out_ref, own_ref,
    pgs, pool_v, send_v, kv_v, qbuf, span_v, qaug, kaug, vt, m_ref, acc, s0, s1, x0, x1, obuf, own_v,
    loc_sem, q_send, q_recv, sp_send, sp_recv, pl_send, pl_recv, o_send, o_recv,
):
    me = lax.axis_index("pool")
    ctx = lax.axis_index("cp")
    head = ctx % 4
    my_cols = pl.ds(pl.multiple_of(head * HEAD_DIM, HEAD_DIM), HEAD_DIM)

    def group_cols(index):
        return pl.ds(pl.multiple_of(index * COLS, COLS), COLS)

    local = [
        pltpu.make_async_copy(pk_ref.at[:, :, my_cols], pool_v.at[0], loc_sem.at[0]),
        pltpu.make_async_copy(pv_ref.at[:, :, my_cols], pool_v.at[1], loc_sem.at[1]),
        pltpu.make_async_copy(q_ref.at[0, :, group_cols(head)], qbuf.at[0], loc_sem.at[2]),
        pltpu.make_async_copy(sk_ref.at[0, :, my_cols], span_v.at[0, 0], loc_sem.at[3]),
        pltpu.make_async_copy(sv_ref.at[0, :, my_cols], span_v.at[0, 1], loc_sem.at[4]),
    ]
    for copy in local:
        copy.start()

    barrier = pltpu.get_barrier_semaphore()
    for k in range(1, 16):
        pl.semaphore_signal(barrier, inc=1, device_id=(xor(me, k), ctx), device_id_type=MESH)
    for k in range(1, 8):
        pl.semaphore_signal(barrier, inc=1, device_id=(me, xor(ctx, k)), device_id_type=MESH)

    base = me * PAGES_DEV

    def scan(r, _):
        live = npages[r]
        first = jnp.int32(0)
        second = jnp.int32(0)
        for s in range(SLOTS):
            page = pid[r, s] - base
            hit = (page >= 0) & (page < PAGES_DEV) & (s < live)
            second = jnp.where(hit, first, second)
            first = jnp.where(hit, page, first)
        pgs[r, 0] = first
        pgs[r, 1] = second
        return 0

    lax.fori_loop(0, 16, scan, 0)
    pl.semaphore_wait(barrier, 22)

    q_copies = {}
    for slot in (1, 2, 3):
        mate = xor(ctx, BLOCK_XOR[slot])
        q_copies[slot] = pltpu.make_async_remote_copy(
            src_ref=q_ref.at[0, :, group_cols(mate % 4)], dst_ref=qbuf.at[slot],
            send_sem=q_send.at[slot], recv_sem=q_recv.at[slot],
            device_id=(me, mate), device_id_type=MESH)
        q_copies[slot].start()

    local[0].wait()
    local[1].wait()

    def pick(k, dst):
        r = xor(me, k)
        for cap in range(2):
            page = pgs[r, cap]
            dst[k, 0, cap] = pool_v[0, page]
            dst[k, 1, cap] = pool_v[1, page]

    pool_copies = {}
    for k in SEND_ORDER:
        pool_copies[k] = pltpu.make_async_remote_copy(
            src_ref=send_v.at[k], dst_ref=kv_v.at[k],
            send_sem=pl_send.at[k], recv_sem=pl_recv.at[k],
            device_id=(xor(me, k), ctx), device_id_type=MESH)
    pick(SEND_ORDER[0], send_v)
    for now, after in zip(SEND_ORDER, SEND_ORDER[1:] + (None,)):
        if after is not None:
            pick(after, send_v)
        else:
            pick(0, kv_v)
        pool_copies[now].start()

    span_copies = {}
    for k in (1, 3, 2, 4, 5, 7, 6):
        mate = xor(ctx, k)
        cols = pl.ds(pl.multiple_of((mate % 4) * HEAD_DIM, HEAD_DIM), HEAD_DIM)
        for which, ref in ((0, sk_ref), (1, sv_ref)):
            span_copies[k, which] = pltpu.make_async_remote_copy(
                src_ref=ref.at[0, :, cols], dst_ref=span_v.at[k, which],
                send_sem=sp_send.at[k, which], recv_sem=sp_recv.at[k, which],
                device_id=(me, mate), device_id_type=MESH)
            span_copies[k, which].start()

    row_iota = lax.broadcasted_iota(jnp.int32, (TOK, TOK), 0)
    col_iota = lax.broadcasted_iota(jnp.int32, (TOK, TOK), 1)
    eye = jnp.where(row_iota == col_iota, 1.0, 0.0).astype(F32).astype(BF16)
    later = jnp.where(row_iota > col_iota, NEG, 0.0).astype(F32).astype(BF16)
    for slot in range(4):
        for g in range(GROUPS):
            qaug[slot, g * TOK:(g + 1) * TOK, HEAD_DIM:] = eye
    for slot in range(4):
        for k in range(8):
            if BLOCK_XOR[slot] == k:
                mask = later
            else:
                hidden = xor(ctx, k) > xor(ctx, BLOCK_XOR[slot])
                mask = jnp.full((TOK, TOK), jnp.where(hidden, NEG, 0.0), F32).astype(BF16)
            kaug[4 + slot, k * TOK:(k + 1) * TOK, HEAD_DIM:] = mask
    my_ids = ids_ref[pl.ds(me, 1), :]
    slot_iota = lax.broadcasted_iota(jnp.int32, (1, SLOTS), 1)
    my_ids = jnp.where(slot_iota < npages[me], my_ids, -1)
    for j, owners in enumerate(CHUNK_OWNERS):
        for i, k in enumerate(owners):
            low = xor(me, k) * PAGES_DEV
            held = jnp.where((my_ids >= low) & (my_ids < low + PAGES_DEV), 1.0, 0.0).astype(F32)
            count = jnp.sum(held, axis=1, keepdims=True)
            for cap in range(2):
                bias = jnp.where(count > cap + 0.5, 0.0, NEG)
                at = (2 * i + cap) * TOK
                kaug[j, at:at + TOK, HEAD_DIM:] = jnp.broadcast_to(bias, (TOK, TOK)).astype(BF16)
    vt[:, HEAD_DIM:, :] = jnp.ones((5, VROWS - HEAD_DIM, KEYS), BF16)
    m_ref[...] = jnp.full(m_ref.shape, NEG, F32)
    acc[...] = jnp.zeros(acc.shape, F32)
    s1[...] = jnp.full(s1.shape, NEG, F32)
    x1[...] = jnp.full(x1.shape, NEG, F32)

    def load_block(slot):
        for g in range(GROUPS):
            qaug[slot, g * TOK:(g + 1) * TOK, :HEAD_DIM] = qbuf[slot, :, g * HEAD_DIM:(g + 1) * HEAD_DIM]

    def load_values(chunk, i, values):
        vt[chunk, :HEAD_DIM, i * TOK:(i + 1) * TOK] = values.astype(F32).T.astype(BF16)

    def load_prefix(j):
        for i, k in enumerate(CHUNK_OWNERS[j]):
            if k:
                pool_copies[k].wait_recv()
        for i, k in enumerate(CHUNK_OWNERS[j]):
            for cap in range(2):
                at = (2 * i + cap) * TOK
                kaug[j, at:at + TOK, :HEAD_DIM] = kv_v[k, 0, cap]
                load_values(j + (j > 1), 2 * i + cap, kv_v[k, 1, cap])

    def load_span():
        local[3].wait()
        local[4].wait()
        for k in range(1, 8):
            span_copies[k, 0].wait_recv()
            span_copies[k, 1].wait_recv()
        for k in range(8):
            for slot in range(4):
                kaug[4 + slot, k * TOK:(k + 1) * TOK, :HEAD_DIM] = span_v[k, 0]
            load_values(2, k, span_v[k, 1])

    def scores(chunk, block, half, s_ref, x_ref):
        at = jnp.where(chunk == 2, 4 + block, jnp.where(chunk > 2, chunk - 1, chunk))
        s = lax.dot_general(
            kaug[at], qaug[block, half * ROWS:(half + 1) * ROWS, :],
            (((1,), (1,)), ((), ())), preferred_element_type=F32)
        s_ref[...] = s
        x_ref[...] = jnp.max(s, axis=0, keepdims=True)

    def absorb(chunk, block, half, s_ref, x_ref):
        t = block * 2 + half
        m_old = m_ref[t]
        m_new = jnp.maximum(m_old, x_ref[...])
        alpha = jnp.exp2((m_old - m_new) * SCALE2)
        p = jnp.exp2((s_ref[...] - m_new) * SCALE2).astype(BF16)
        m_ref[t] = m_new
        acc[t] = acc[t] * alpha + jnp.dot(vt[chunk], p, preferred_element_type=F32)

    def body(now, before):
        scores(*now, 0, s0, x0)
        absorb(*before, 1, s1, x1)
        scores(*now, 1, s1, x1)
        absorb(*now, 0, s0, x0)

    def result(block, g):
        a = acc.at[block * 2 + g // 4]
        cols = slice(g % 4 * TOK, (g % 4 + 1) * TOK)
        return (a[:HEAD_DIM, cols] / a[HEAD_DIM:HEAD_DIM + 1, cols]).T

    local[2].wait()
    load_block(0)
    load_prefix(0)

    def step(u, _):
        for at, slot in ((1, 1), (2, 2), (6, 3)):
            @pl.when(u == at)
            def _():
                q_copies[slot].wait_recv()
                load_block(slot)

        @pl.when(u == 3)
        def _():
            load_prefix(1)

        @pl.when(u == 8)
        def _():
            load_span()

        @pl.when(u == 12)
        def _():
            load_prefix(2)

        @pl.when(u == 16)
        def _():
            load_prefix(3)

        body(schedule(u), schedule(jnp.maximum(u - 1, 0)))
        return 0

    lax.fori_loop(0, 17, step, 0)

    o_copies = []
    for block in (3, 2, 1):
        body((4, block - 1), (4, block))
        for g in range(GROUPS):
            obuf[block, :, g * HEAD_DIM:(g + 1) * HEAD_DIM] = result(block, g).astype(BF16)
        mate = xor(ctx, BLOCK_XOR[block])
        copy = pltpu.make_async_remote_copy(
            src_ref=obuf.at[block], dst_ref=out_ref.at[:, group_cols(head)],
            send_sem=o_send.at[block], recv_sem=o_recv.at[block],
            device_id=(me, mate), device_id_type=MESH)
        copy.start()
        o_copies.append(copy)
    absorb(4, 0, 1, s1, x1)
    for g in range(GROUPS):
        own_v[:, g * HEAD_DIM:(g + 1) * HEAD_DIM] = result(0, g)
    own_copy = pltpu.make_async_copy(own_v, own_ref, loc_sem.at[5])
    own_copy.start()

    for copies in (q_copies.values(), span_copies.values(), pool_copies.values()):
        for copy in copies:
            copy.wait_send()
    for copy in o_copies:
        copy.wait()
    own_copy.wait()


def attend(queries, span_keys, span_values, pool_keys, pool_values, page_ids, prefix_pages):
    vmem = pl.BlockSpec(memory_space=pltpu.VMEM)
    smem = pl.BlockSpec(memory_space=pltpu.SMEM)
    hbm = pl.BlockSpec(memory_space=pl.ANY)
    dma = pltpu.SemaphoreType.DMA
    far, own = pl.pallas_call(
        kernel,
        out_shape=(
            jax.ShapeDtypeStruct((TOK, HEADS * HEAD_DIM), BF16),
            jax.ShapeDtypeStruct((TOK, COLS), F32),
        ),
        in_specs=[smem, smem, vmem, hbm, hbm, hbm, hbm, hbm],
        out_specs=(hbm, hbm),
        scratch_shapes=[
            pltpu.SMEM((16, 2), jnp.int32),
            pltpu.VMEM((2, PAGES_DEV, TOK, HEAD_DIM), BF16),
            pltpu.VMEM((16, 2, 2, TOK, HEAD_DIM), BF16),
            pltpu.VMEM((16, 2, 2, TOK, HEAD_DIM), BF16),
            pltpu.VMEM((4, TOK, COLS), BF16),
            pltpu.VMEM((8, 2, TOK, HEAD_DIM), BF16),
            pltpu.VMEM((4, GROUPS * TOK, 2 * HEAD_DIM), BF16),
            pltpu.VMEM((8, KEYS, 2 * HEAD_DIM), BF16),
            pltpu.VMEM((5, VROWS, KEYS), BF16),
            pltpu.VMEM((8, 1, ROWS), F32),
            pltpu.VMEM((8, VROWS, ROWS), F32),
            pltpu.VMEM((KEYS, ROWS), F32),
            pltpu.VMEM((KEYS, ROWS), F32),
            pltpu.VMEM((1, ROWS), F32),
            pltpu.VMEM((1, ROWS), F32),
            pltpu.VMEM((4, TOK, COLS), BF16),
            pltpu.VMEM((TOK, COLS), F32),
            dma((6,)),
            dma((4,)), dma((4,)),
            dma((8, 2)), dma((8, 2)),
            dma((16,)), dma((16,)),
            dma((4,)), dma((4,)),
        ],
        compiler_params=pltpu.CompilerParams(
            collective_id=0, has_side_effects=True, vmem_limit_bytes=64000 * 1024),
        name="attend",
    )(page_ids, prefix_pages, page_ids, queries, span_keys, span_values, pool_keys, pool_values)
    start = lax.axis_index("cp") % 4 * COLS
    attended = lax.dynamic_update_slice(far.astype(F32), own, (0, start))
    return attended[None]


def solution(mesh):
    in_specs = (
        P("pool", "cp", None),
        P("pool", "cp", None),
        P("pool", "cp", None),
        P("pool", None, None),
        P("pool", None, None),
        P(),
        P(),
    )
    out_specs = P("pool", "cp", None)
    return jax.shard_map(attend, mesh=mesh, in_specs=in_specs, out_specs=out_specs, check_vma=False)
```

```python
import functools

import jax
import jax.numpy as jnp
import numpy as np
from jax import lax
from jax.experimental import pallas as pl
from jax.experimental.pallas import tpu as pltpu
from jax.sharding import PartitionSpec as P

HEAD_DIM = 128
HEADS = 32
KV_HEADS = 4
PAGES_DEV = 24
SLOTS = 32
TOK = 128
GROUPS = HEADS // KV_HEADS
COLS = GROUPS * HEAD_DIM

ROWS = 512
KEYS = 1024
VROWS = 144
NEG = -1e30
SCALE2 = float(HEAD_DIM**-0.5 * np.log2(np.e))
MESH = pl.DeviceIdType.MESH

CHUNK_OWNERS = ((0, 1, 2, 6), (3, 7, 8, 9), (10, 11, 14, 15), (4, 5, 12, 13))
WAVES = ((1, 2, 6, 8, 9), (3, 7, 10, 14), (11, 15), (4, 12, 5, 13))
OTHER_X = (9, 11, 13, 15)
BLOCK_XOR = (0, 1, 3, 2)
BF16 = jnp.bfloat16
F32 = jnp.float32
SPAN, LAST = 3, 4


def xor(index, offset):
    for bit in range(4):
        if offset >> bit & 1:
            index = index + (1 << bit) * (1 - 2 * ((index // (1 << bit)) % 2))
    return index


def xor_block(index, block):
    low = jnp.where(block == 3, 0, 1)
    high = jnp.where(block == 1, 0, 1)
    index = index + low * (1 - 2 * (index % 2))
    return index + 2 * high * (1 - 2 * ((index // 2) % 2))


def schedule(u):
    chunk = jnp.where(u < 9, u // 3, u - 9)
    block = jnp.where(u < 9, u % 3, 3)
    return chunk, block


def kernel(
    pid, npages, ids_ref, q_ref, sk_ref, sv_ref, pk_ref, pv_ref,
    out_ref, own_ref,
    pgs, pool_v, send_v, kv_v, qbuf, span_v, qaug, kaug, vt, m_ref, acc, s0, s1, x0, x1, obuf, own_v,
    loc_sem, q_send, q_recv, sp_send, sp_recv, pl_send, pl_recv, o_send, o_recv,
):
    me = lax.axis_index("pool")
    ctx = lax.axis_index("cp")
    head = ctx % 4
    my_cols = pl.ds(pl.multiple_of(head * HEAD_DIM, HEAD_DIM), HEAD_DIM)

    def group_cols(index):
        return pl.ds(pl.multiple_of(index * COLS, COLS), COLS)

    local = [
        pltpu.make_async_copy(pk_ref.at[:, :, my_cols], pool_v.at[0], loc_sem.at[0]),
        pltpu.make_async_copy(pv_ref.at[:, :, my_cols], pool_v.at[1], loc_sem.at[1]),
        pltpu.make_async_copy(q_ref.at[0, :, group_cols(head)], qbuf.at[0], loc_sem.at[2]),
        pltpu.make_async_copy(sk_ref.at[0, :, my_cols], span_v.at[0, 0], loc_sem.at[3]),
        pltpu.make_async_copy(sv_ref.at[0, :, my_cols], span_v.at[0, 1], loc_sem.at[4]),
    ]
    for copy in local:
        copy.start()

    barrier = pltpu.get_barrier_semaphore()
    other = xor(ctx, 4)
    for k in range(1, 16):
        pl.semaphore_signal(
            barrier, inc=1, device_id=(xor(me, k), other if k in OTHER_X else ctx), device_id_type=MESH)
    for k in range(1, 8):
        pl.semaphore_signal(barrier, inc=1, device_id=(me, xor(ctx, k)), device_id_type=MESH)

    base = me * PAGES_DEV

    def scan(r, _):
        live = npages[r]
        first = jnp.int32(0)
        second = jnp.int32(0)
        for s in range(SLOTS):
            page = pid[r, s] - base
            hit = (page >= 0) & (page < PAGES_DEV) & (s < live)
            second = jnp.where(hit, first, second)
            first = jnp.where(hit, page, first)
        pgs[r, 0] = first
        pgs[r, 1] = second
        return 0

    lax.fori_loop(0, 16, scan, 0)
    pl.semaphore_wait(barrier, 22)

    q_copies = {}
    for slot in (1, 2, 3):
        mate = xor(ctx, BLOCK_XOR[slot])
        q_copies[slot] = pltpu.make_async_remote_copy(
            src_ref=q_ref.at[0, :, group_cols(mate % 4)], dst_ref=qbuf.at[slot],
            send_sem=q_send.at[slot], recv_sem=q_recv.at[slot],
            device_id=(me, mate), device_id_type=MESH)
    q_copies[1].start()
    q_copies[2].start()

    local[0].wait()
    local[1].wait()

    def pick(k, dst):
        r = xor(me, k)
        for cap in range(2):
            page = pgs[r, cap]
            dst[k, 0, cap] = pool_v[0, page]
            dst[k, 1, cap] = pool_v[1, page]

    pool_copies = {}
    for k in range(1, 16):
        pool_copies[k] = pltpu.make_async_remote_copy(
            src_ref=send_v.at[k], dst_ref=kv_v.at[k],
            send_sem=pl_send.at[k], recv_sem=pl_recv.at[k],
            device_id=(xor(me, k), other if k in OTHER_X else ctx), device_id_type=MESH)

    def send_pages(wave):
        for k in WAVES[wave]:
            pool_copies[k].start()

    for k in WAVES[0]:
        pick(k, send_v)
    pick(0, kv_v)
    send_pages(0)
    for wave in WAVES[1:]:
        for k in wave:
            pick(k, send_v)

    span_copies = {}
    for k in range(1, 8):
        mate = xor(ctx, k)
        cols = pl.ds(pl.multiple_of((mate % 4) * HEAD_DIM, HEAD_DIM), HEAD_DIM)
        for which, ref in ((0, sk_ref), (1, sv_ref)):
            span_copies[k, which] = pltpu.make_async_remote_copy(
                src_ref=ref.at[0, :, cols], dst_ref=span_v.at[k, which],
                send_sem=sp_send.at[k, which], recv_sem=sp_recv.at[k, which],
                device_id=(me, mate), device_id_type=MESH)

    def send_span():
        for k in (1, 3, 2):
            span_copies[k, 0].start()
            span_copies[k, 1].start()

        @pl.when(ctx < 4)
        def _():
            for k in (4, 5, 7, 6):
                span_copies[k, 0].start()
                span_copies[k, 1].start()

    row_iota = lax.broadcasted_iota(jnp.int32, (TOK, TOK), 0)
    col_iota = lax.broadcasted_iota(jnp.int32, (TOK, TOK), 1)
    eye = jnp.where(row_iota == col_iota, 1.0, 0.0).astype(F32).astype(BF16)
    later = jnp.where(row_iota > col_iota, NEG, 0.0).astype(F32).astype(BF16)
    for slot in range(4):
        for g in range(GROUPS):
            qaug[slot, g * TOK:(g + 1) * TOK, HEAD_DIM:] = eye
    for slot in range(4):
        for k in range(8):
            if BLOCK_XOR[slot] == k:
                mask = later
            else:
                hidden = xor(ctx, k) > xor(ctx, BLOCK_XOR[slot])
                mask = jnp.full((TOK, TOK), jnp.where(hidden, NEG, 0.0), F32).astype(BF16)
            kaug[4 + slot, k * TOK:(k + 1) * TOK, HEAD_DIM:] = mask
    my_ids = ids_ref[pl.ds(me, 1), :]
    slot_iota = lax.broadcasted_iota(jnp.int32, (1, SLOTS), 1)
    my_ids = jnp.where(slot_iota < npages[me], my_ids, -1)
    for j, owners in enumerate(CHUNK_OWNERS):
        for i, k in enumerate(owners):
            low = xor(me, k) * PAGES_DEV
            held = jnp.where((my_ids >= low) & (my_ids < low + PAGES_DEV), 1.0, 0.0).astype(F32)
            count = jnp.sum(held, axis=1, keepdims=True)
            for cap in range(2):
                bias = jnp.where(count > cap + 0.5, 0.0, NEG)
                at = (2 * i + cap) * TOK
                kaug[j, at:at + TOK, HEAD_DIM:] = jnp.broadcast_to(bias, (TOK, TOK)).astype(BF16)
    vt[:, HEAD_DIM:, :] = jnp.ones((5, VROWS - HEAD_DIM, KEYS), BF16)
    m_ref[...] = jnp.full(m_ref.shape, NEG, F32)
    acc[...] = jnp.zeros(acc.shape, F32)
    s1[...] = jnp.full(s1.shape, NEG, F32)
    x1[...] = jnp.full(x1.shape, NEG, F32)

    def load_block(slot):
        for g in range(GROUPS):
            qaug[slot, g * TOK:(g + 1) * TOK, :HEAD_DIM] = qbuf[slot, :, g * HEAD_DIM:(g + 1) * HEAD_DIM]

    def load_values(chunk, i, values):
        vt[chunk, :HEAD_DIM, i * TOK:(i + 1) * TOK] = values.astype(F32).T.astype(BF16)

    def load_prefix(j):
        for i, k in enumerate(CHUNK_OWNERS[j]):
            if k:
                pool_copies[k].wait_recv()
        for i, k in enumerate(CHUNK_OWNERS[j]):
            for cap in range(2):
                at = (2 * i + cap) * TOK
                kaug[j, at:at + TOK, :HEAD_DIM] = kv_v[k, 0, cap]
                load_values(j + (j > 2), 2 * i + cap, kv_v[k, 1, cap])

    def load_span():
        local[3].wait()
        local[4].wait()
        for k in range(1, 4):
            span_copies[k, 0].wait_recv()
            span_copies[k, 1].wait_recv()

        @pl.when(ctx >= 4)
        def _():
            for k in range(4, 8):
                span_copies[k, 0].wait_recv()
                span_copies[k, 1].wait_recv()

        for k in range(8):
            at = jnp.where(ctx < 4, k % 4, k)
            for slot in range(4):
                kaug[4 + slot, k * TOK:(k + 1) * TOK, :HEAD_DIM] = span_v[at, 0]
            load_values(3, k, span_v[at, 1])

    def scores(chunk, block, half, s_ref, x_ref):
        at = chunk
        if isinstance(chunk, int) and chunk >= SPAN:
            at = 4 + block if chunk == SPAN else 3
        s = lax.dot_general(
            kaug[at], qaug[block, half * ROWS:(half + 1) * ROWS, :],
            (((1,), (1,)), ((), ())), preferred_element_type=F32)
        s_ref[...] = s
        x_ref[...] = jnp.max(s, axis=0, keepdims=True)

    def absorb(chunk, block, half, s_ref, x_ref):
        t = block * 2 + half
        m_old = m_ref[t]
        m_new = jnp.maximum(m_old, x_ref[...])
        alpha = jnp.exp2((m_old - m_new) * SCALE2)
        p = jnp.exp2((s_ref[...] - m_new) * SCALE2).astype(BF16)
        m_ref[t] = m_new
        acc[t] = acc[t] * alpha + jnp.dot(vt[chunk], p, preferred_element_type=F32)

    def body(now, before):
        scores(*now, 0, s0, x0)
        absorb(*before, 1, s1, x1)
        scores(*now, 1, s1, x1)
        absorb(*now, 0, s0, x0)

    def result(block, half, g):
        a = acc.at[block * 2 + half]
        cols = slice(g * TOK, (g + 1) * TOK)
        return (a[:HEAD_DIM, cols] / a[HEAD_DIM:HEAD_DIM + 1, cols]).T

    def out_copy(block, half):
        mate = xor_block(ctx, block)
        cols = pl.ds(pl.multiple_of(head * COLS + half * (COLS // 2), COLS // 2), COLS // 2)
        return pltpu.make_async_remote_copy(
            src_ref=obuf.at[block, half], dst_ref=out_ref.at[:, cols],
            send_sem=o_send.at[block, half], recv_sem=o_recv.at[block, half],
            device_id=(me, mate), device_id_type=MESH)

    def send(block, half):
        for g in range(4):
            obuf[block, half, :, g * HEAD_DIM:(g + 1) * HEAD_DIM] = result(block, half, g).astype(BF16)
        out_copy(block, half).start()

    def keep(half):
        for g in range(4):
            at = (half * 4 + g) * HEAD_DIM
            own_v[:, at:at + HEAD_DIM] = result(0, half, g)

    local[2].wait()
    load_block(0)
    for k in WAVES[0]:
        pool_copies[k].wait_send()
    send_pages(1)
    load_prefix(0)

    def step(u, _):
        for at, slot in ((1, 1), (2, 2), (9, 3)):
            @pl.when(u == at)
            def _():
                q_copies[slot].wait_recv()
                load_block(slot)

        for at, j in ((3, 1), (6, 2)):
            @pl.when(u == at)
            def _():
                load_prefix(j)

        @pl.when(u == 1)
        def _():
            send_pages(2)
            q_copies[3].start()

        @pl.when(u == 2)
        def _():
            send_span()

        @pl.when(u == 3)
        def _():
            send_pages(3)

        body(schedule(u), schedule(jnp.maximum(u - 1, 0)))
        return 0

    lax.fori_loop(0, 12, step, 0)
    load_span()
    body((SPAN, 3), (2, 3))
    body((SPAN, 2), (SPAN, 3))
    load_prefix(3)
    body((LAST, 3), (SPAN, 2))
    send(3, 0)
    body((LAST, 2), (LAST, 3))
    send(3, 1)
    send(2, 0)
    body((SPAN, 1), (LAST, 2))
    send(2, 1)
    body((LAST, 1), (SPAN, 1))
    send(1, 0)
    body((SPAN, 0), (LAST, 1))
    send(1, 1)
    body((LAST, 0), (SPAN, 0))
    keep(0)
    absorb(LAST, 0, 1, s1, x1)
    keep(1)
    own_copy = pltpu.make_async_copy(own_v, own_ref, loc_sem.at[5])
    own_copy.start()

    for slot in (1, 2, 3):
        q_copies[slot].wait_send()
    for wave in WAVES[1:]:
        for k in wave:
            pool_copies[k].wait_send()
    for k in range(1, 4):
        span_copies[k, 0].wait_send()
        span_copies[k, 1].wait_send()

    @pl.when(ctx < 4)
    def _():
        for k in range(4, 8):
            span_copies[k, 0].wait_send()
            span_copies[k, 1].wait_send()

    for block in (3, 2, 1):
        for half in range(2):
            out_copy(block, half).wait()
    own_copy.wait()


def attend(queries, span_keys, span_values, pool_keys, pool_values, page_ids, prefix_pages):
    vmem = pl.BlockSpec(memory_space=pltpu.VMEM)
    smem = pl.BlockSpec(memory_space=pltpu.SMEM)
    hbm = pl.BlockSpec(memory_space=pl.ANY)
    dma = pltpu.SemaphoreType.DMA
    far, own = pl.pallas_call(
        kernel,
        out_shape=(
            jax.ShapeDtypeStruct((TOK, HEADS * HEAD_DIM), BF16),
            jax.ShapeDtypeStruct((TOK, COLS), F32),
        ),
        in_specs=[smem, smem, vmem, hbm, hbm, hbm, hbm, hbm],
        out_specs=(hbm, hbm),
        scratch_shapes=[
            pltpu.SMEM((16, 2), jnp.int32),
            pltpu.VMEM((2, PAGES_DEV, TOK, HEAD_DIM), BF16),
            pltpu.VMEM((16, 2, 2, TOK, HEAD_DIM), BF16),
            pltpu.VMEM((16, 2, 2, TOK, HEAD_DIM), BF16),
            pltpu.VMEM((4, TOK, COLS), BF16),
            pltpu.VMEM((8, 2, TOK, HEAD_DIM), BF16),
            pltpu.VMEM((4, GROUPS * TOK, 2 * HEAD_DIM), BF16),
            pltpu.VMEM((8, KEYS, 2 * HEAD_DIM), BF16),
            pltpu.VMEM((5, VROWS, KEYS), BF16),
            pltpu.VMEM((8, 1, ROWS), F32),
            pltpu.VMEM((8, VROWS, ROWS), F32),
            pltpu.VMEM((KEYS, ROWS), F32),
            pltpu.VMEM((KEYS, ROWS), F32),
            pltpu.VMEM((1, ROWS), F32),
            pltpu.VMEM((1, ROWS), F32),
            pltpu.VMEM((4, 2, TOK, COLS // 2), BF16),
            pltpu.VMEM((TOK, COLS), F32),
            dma((6,)),
            dma((4,)), dma((4,)),
            dma((8, 2)), dma((8, 2)),
            dma((16,)), dma((16,)),
            dma((4, 2)), dma((4, 2)),
        ],
        compiler_params=pltpu.CompilerParams(
            collective_id=0, has_side_effects=True, vmem_limit_bytes=64000 * 1024),
        name="attend",
    )(page_ids, prefix_pages, page_ids, queries, span_keys, span_values, pool_keys, pool_values)
    start = lax.axis_index("cp") % 4 * COLS
    attended = lax.dynamic_update_slice(far.astype(F32), own, (0, start))
    return attended[None]


def solution(mesh):
    in_specs = (
        P("pool", "cp", None),
        P("pool", "cp", None),
        P("pool", "cp", None),
        P("pool", None, None),
        P("pool", None, None),
        P(),
        P(),
    )
    out_specs = P("pool", "cp", None)
    return jax.shard_map(attend, mesh=mesh, in_specs=in_specs, out_specs=out_specs, check_vma=False)
```

```python
import functools

import jax
import jax.numpy as jnp
import numpy as np
from jax import lax
from jax.experimental import pallas as pl
from jax.experimental.pallas import tpu as pltpu
from jax.sharding import PartitionSpec as P

HEAD_DIM = 128
HEADS = 32
KV_HEADS = 4
PAGES_DEV = 24
SLOTS = 32
TOK = 128
GROUPS = HEADS // KV_HEADS
COLS = GROUPS * HEAD_DIM

ROWS = 512
KEYS = 1024
VROWS = 144
NEG = -1e30
SCALE2 = float(HEAD_DIM**-0.5 * np.log2(np.e))
MESH = pl.DeviceIdType.MESH

CHUNK_OWNERS = ((0, 1, 8, 9), (2, 3, 6, 7), (10, 11, 14, 15), (4, 5, 12, 13))
WAVES = ((8, 9, 1, 2, 6, 3, 7), (4, 12), (10, 14, 11, 15))
FAR = (4, 12)
OTHER_X = (9, 11, 15)
BLOCK_XOR = (0, 1, 3, 2)
BF16 = jnp.bfloat16
F32 = jnp.float32
SPAN, LAST = 3, 4
CONVERT_ROWS = 64


def xor(index, offset):
    for bit in range(4):
        if offset >> bit & 1:
            index = index + (1 << bit) * (1 - 2 * ((index // (1 << bit)) % 2))
    return index


def xor_block(index, block):
    low = jnp.where(block == 3, 0, 1)
    high = jnp.where(block == 1, 0, 1)
    index = index + low * (1 - 2 * (index % 2))
    return index + 2 * high * (1 - 2 * ((index // 2) % 2))


def schedule(u):
    chunk = jnp.where(u < 6, u // 3, jnp.where(u < 8, u - 6, SPAN))
    block = jnp.where(u < 6, u % 3, jnp.where(u < 8, 3, u - 8))
    return chunk, block


def kernel(
    pid, npages, ids_ref, q_ref, sk_ref, sv_ref, pk_ref, pv_ref,
    out_ref, own_ref,
    pgs, pool_v, send_v, kv_v, qbuf, span_v, qaug, kaug, vt, m_ref, acc, s0, s1, x0, x1, obuf, own_v,
    loc_sem, q_send, q_recv, sp_send, sp_recv, pl_send, pl_recv, o_send, o_recv,
):
    me = lax.axis_index("pool")
    ctx = lax.axis_index("cp")
    head = ctx % 4
    my_cols = pl.ds(pl.multiple_of(head * HEAD_DIM, HEAD_DIM), HEAD_DIM)

    def group_cols(index):
        return pl.ds(pl.multiple_of(index * COLS, COLS), COLS)

    local = [
        pltpu.make_async_copy(pk_ref.at[:, :, my_cols], pool_v.at[0], loc_sem.at[0]),
        pltpu.make_async_copy(pv_ref.at[:, :, my_cols], pool_v.at[1], loc_sem.at[1]),
        pltpu.make_async_copy(q_ref.at[0, :, group_cols(head)], qbuf.at[0], loc_sem.at[2]),
        pltpu.make_async_copy(sk_ref.at[0, :, my_cols], span_v.at[0, 0], loc_sem.at[3]),
        pltpu.make_async_copy(sv_ref.at[0, :, my_cols], span_v.at[0, 1], loc_sem.at[4]),
    ]
    for copy in local:
        copy.start()

    barrier = pltpu.get_barrier_semaphore()
    other = xor(ctx, 4)
    later_half = ctx // 4

    def owner(k):
        index = xor(me, k)
        return index + later_half * (1 - 2 * (index % 2)) if k in FAR else index

    def slot_of(k):
        return k + later_half if k in FAR else k

    for wave in WAVES:
        for k in wave:
            pl.semaphore_signal(
                barrier, inc=1, device_id=(owner(k), other if k in OTHER_X else ctx), device_id_type=MESH)
    for k in range(1, 8):
        pl.semaphore_signal(barrier, inc=1, device_id=(me, xor(ctx, k)), device_id_type=MESH)

    base = me * PAGES_DEV

    def scan(r, _):
        live = npages[r]
        first = jnp.int32(0)
        second = jnp.int32(0)
        for s in range(SLOTS):
            page = pid[r, s] - base
            hit = (page >= 0) & (page < PAGES_DEV) & (s < live)
            second = jnp.where(hit, first, second)
            first = jnp.where(hit, page, first)
        pgs[r, 0] = first
        pgs[r, 1] = second
        return 0

    lax.fori_loop(0, 16, scan, 0)
    pl.semaphore_wait(barrier, sum(map(len, WAVES)) + 7)

    q_copies = {}
    for slot in (1, 2, 3):
        mate = xor(ctx, BLOCK_XOR[slot])
        q_copies[slot] = pltpu.make_async_remote_copy(
            src_ref=q_ref.at[0, :, group_cols(mate % 4)], dst_ref=qbuf.at[slot],
            send_sem=q_send.at[slot], recv_sem=q_recv.at[slot],
            device_id=(me, mate), device_id_type=MESH)
    q_copies[1].start()
    q_copies[2].start()

    local[0].wait()
    local[1].wait()

    def pick(k, dst):
        r = owner(k)
        slot = slot_of(k)
        for cap in range(2):
            page = pgs[r, cap]
            dst[slot, 0, cap] = pool_v[0, page]
            dst[slot, 1, cap] = pool_v[1, page]

    pool_copies = {}
    for wave in WAVES:
        for k in wave:
            slot = slot_of(k)
            pool_copies[k] = pltpu.make_async_remote_copy(
                src_ref=send_v.at[slot], dst_ref=kv_v.at[slot],
                send_sem=pl_send.at[slot], recv_sem=pl_recv.at[slot],
                device_id=(owner(k), other if k in OTHER_X else ctx), device_id_type=MESH)

    def passed_on(k, slot):
        return pltpu.make_async_remote_copy(
            src_ref=kv_v.at[slot], dst_ref=kv_v.at[slot],
            send_sem=pl_send.at[2 * k + 1 - slot], recv_sem=pl_recv.at[slot],
            device_id=(me, other), device_id_type=MESH)

    def pass_on():
        for k in FAR:
            pool_copies[k].wait_recv()
            passed_on(k, slot_of(k)).start()

    def send_pages(wave):
        for k in WAVES[wave]:
            pool_copies[k].start()

    for k in WAVES[0]:
        pick(k, send_v)
    pick(0, kv_v)
    send_pages(0)
    for wave in WAVES[1:]:
        for k in wave:
            pick(k, send_v)

    span_copies = {}
    for k in range(1, 8):
        mate = xor(ctx, k)
        cols = pl.ds(pl.multiple_of((mate % 4) * HEAD_DIM, HEAD_DIM), HEAD_DIM)
        for which, ref in ((0, sk_ref), (1, sv_ref)):
            span_copies[k, which] = pltpu.make_async_remote_copy(
                src_ref=ref.at[0, :, cols], dst_ref=span_v.at[k, which],
                send_sem=sp_send.at[k, which], recv_sem=sp_recv.at[k, which],
                device_id=(me, mate), device_id_type=MESH)

    def send_span():
        for k in (1, 3, 2):
            span_copies[k, 0].start()
            span_copies[k, 1].start()

        @pl.when(ctx < 4)
        def _():
            for k in (4, 5, 7, 6):
                span_copies[k, 0].start()
                span_copies[k, 1].start()

    row_iota = lax.broadcasted_iota(jnp.int32, (TOK, TOK), 0)
    col_iota = lax.broadcasted_iota(jnp.int32, (TOK, TOK), 1)
    eye = jnp.where(row_iota == col_iota, 1.0, 0.0).astype(F32).astype(BF16)
    later = jnp.where(row_iota > col_iota, NEG, 0.0).astype(F32).astype(BF16)
    for slot in range(4):
        for g in range(GROUPS):
            qaug[slot, g * TOK:(g + 1) * TOK, HEAD_DIM:] = eye
    for slot in range(4):
        for k in range(8):
            if BLOCK_XOR[slot] == k:
                mask = later
            else:
                hidden = xor(ctx, k) > xor(ctx, BLOCK_XOR[slot])
                mask = jnp.full((TOK, TOK), jnp.where(hidden, NEG, 0.0), F32).astype(BF16)
            kaug[4 + slot, k * TOK:(k + 1) * TOK, HEAD_DIM:] = mask
    my_ids = ids_ref[pl.ds(me, 1), :]
    slot_iota = lax.broadcasted_iota(jnp.int32, (1, SLOTS), 1)
    my_ids = jnp.where(slot_iota < npages[me], my_ids, -1)
    for j, owners in enumerate(CHUNK_OWNERS):
        for i, k in enumerate(owners):
            low = xor(me, k) * PAGES_DEV
            held = jnp.where((my_ids >= low) & (my_ids < low + PAGES_DEV), 1.0, 0.0).astype(F32)
            count = jnp.sum(held, axis=1, keepdims=True)
            for cap in range(2):
                bias = jnp.where(count > cap + 0.5, 0.0, NEG)
                at = (2 * i + cap) * TOK
                kaug[j, at:at + TOK, HEAD_DIM:] = jnp.broadcast_to(bias, (TOK, TOK)).astype(BF16)
    vt[:, HEAD_DIM:, :] = jnp.ones((5, VROWS - HEAD_DIM, KEYS), BF16)
    m_ref[...] = jnp.full(m_ref.shape, NEG, F32)
    acc[...] = jnp.zeros(acc.shape, F32)
    s1[...] = jnp.full(s1.shape, NEG, F32)
    x1[...] = jnp.full(x1.shape, NEG, F32)

    def load_block(slot):
        for g in range(GROUPS):
            qaug[slot, g * TOK:(g + 1) * TOK, :HEAD_DIM] = qbuf[slot, :, g * HEAD_DIM:(g + 1) * HEAD_DIM]

    def load_values(chunk, i, values):
        vt[chunk, :HEAD_DIM, i * TOK:(i + 1) * TOK] = values.astype(F32).T.astype(BF16)

    def load_prefix(j):
        for i, k in enumerate(CHUNK_OWNERS[j]):
            if k in FAR:
                passed_on(k, k + 1 - later_half).wait_recv()
            elif k and k - 1 not in FAR:
                pool_copies[k].wait_recv()
        for i, k in enumerate(CHUNK_OWNERS[j]):
            for cap in range(2):
                at = (2 * i + cap) * TOK
                kaug[j, at:at + TOK, :HEAD_DIM] = kv_v[k, 0, cap]
                load_values(j + (j > 2), 2 * i + cap, kv_v[k, 1, cap])

    def load_span():
        local[3].wait()
        local[4].wait()
        for k in range(1, 4):
            span_copies[k, 0].wait_recv()
            span_copies[k, 1].wait_recv()

        @pl.when(ctx >= 4)
        def _():
            for k in range(4, 8):
                span_copies[k, 0].wait_recv()
                span_copies[k, 1].wait_recv()

        for k in range(8):
            at = jnp.where(ctx < 4, k % 4, k)
            for slot in range(4):
                kaug[4 + slot, k * TOK:(k + 1) * TOK, :HEAD_DIM] = span_v[at, 0]
            load_values(3, k, span_v[at, 1])

    def scores(chunk, block, half, s_ref, x_ref):
        if isinstance(chunk, int):
            at = 3 if chunk == LAST else chunk
        else:
            at = jnp.where(chunk == SPAN, 4 + block, chunk)
        s = lax.dot_general(
            kaug[at], qaug[block, half * ROWS:(half + 1) * ROWS, :],
            (((1,), (1,)), ((), ())), preferred_element_type=F32)
        s_ref[...] = s
        x_ref[...] = jnp.max(s, axis=0, keepdims=True)

    def absorb(chunk, block, half, s_ref, x_ref):
        t = block * 2 + half
        m_old = m_ref[t]
        m_new = jnp.maximum(m_old, x_ref[...])
        alpha = jnp.exp2((m_old - m_new) * SCALE2)
        p = jnp.exp2((s_ref[...] - m_new) * SCALE2).astype(BF16)
        m_ref[t] = m_new
        acc[t] = acc[t] * alpha + jnp.dot(vt[chunk], p, preferred_element_type=F32)

    def body(now, before):
        scores(*now, 0, s0, x0)
        absorb(*before, 1, s1, x1)
        scores(*now, 1, s1, x1)
        absorb(*now, 0, s0, x0)

    def result(block, half, g):
        a = acc.at[block * 2 + half]
        cols = slice(g * TOK, (g + 1) * TOK)
        return (a[:HEAD_DIM, cols] / a[HEAD_DIM:HEAD_DIM + 1, cols]).T

    def out_copy(block, half):
        mate = xor_block(ctx, block)
        cols = pl.ds(pl.multiple_of(head * COLS + half * (COLS // 2), COLS // 2), COLS // 2)
        return pltpu.make_async_remote_copy(
            src_ref=obuf.at[block, half], dst_ref=out_ref.at[:, cols],
            send_sem=o_send.at[block, half], recv_sem=o_recv.at[block, half],
            device_id=(me, mate), device_id_type=MESH)

    def send(block, half):
        for g in range(4):
            obuf[block, half, :, g * HEAD_DIM:(g + 1) * HEAD_DIM] = result(block, half, g).astype(BF16)
        out_copy(block, half).start()

    def keep(half):
        for g in range(4):
            at = (half * 4 + g) * HEAD_DIM
            own_v[:, at:at + HEAD_DIM] = result(0, half, g)

    local[2].wait()
    load_block(0)
    load_prefix(0)
    send_pages(1)

    def step(u, _):
        @pl.when(u == 8)
        def _():
            pass_on()
            load_span()

        for at, slot in ((1, 1), (2, 2), (6, 3)):
            @pl.when(u == at)
            def _():
                q_copies[slot].wait_recv()
                load_block(slot)

        @pl.when(u == 3)
        def _():
            load_prefix(1)

        @pl.when(u == 1)
        def _():
            q_copies[3].start()

        @pl.when(u == 2)
        def _():
            send_span()

        @pl.when(u == 4)
        def _():
            send_pages(2)

        body(schedule(u), schedule(jnp.maximum(u - 1, 0)))
        return 0

    lax.fori_loop(0, 12, step, 0)

    def finish(i, _):
        block = 3 - i

        @pl.when(i == 0)
        def _():
            load_prefix(2)

        before = jnp.where(i == 0, SPAN, LAST)
        body((2, block), (before, jnp.minimum(block + 1, 3)))

        @pl.when(i > 0)
        def _():
            send(block + 1, 1)

        @pl.when(i == 0)
        def _():
            load_prefix(3)

        body((LAST, block), (2, block))

        @pl.when(i < 3)
        def _():
            send(block, 0)

        return 0

    lax.fori_loop(0, 4, finish, 0)
    keep(0)
    absorb(LAST, 0, 1, s1, x1)
    keep(1)
    own_copy = pltpu.make_async_copy(own_v, own_ref, loc_sem.at[5])
    own_copy.start()

    for slot in (1, 2, 3):
        q_copies[slot].wait_send()
    for wave in WAVES:
        for k in wave:
            pool_copies[k].wait_send()
    for k in FAR:
        passed_on(k, slot_of(k)).wait_send()
    for k in range(1, 4):
        span_copies[k, 0].wait_send()
        span_copies[k, 1].wait_send()

    @pl.when(ctx < 4)
    def _():
        for k in range(4, 8):
            span_copies[k, 0].wait_send()
            span_copies[k, 1].wait_send()

    for block in (3, 2, 1):
        for half in range(2):
            out_copy(block, half).wait()
    own_copy.wait()


def attend(queries, span_keys, span_values, pool_keys, pool_values, page_ids, prefix_pages):
    vmem = pl.BlockSpec(memory_space=pltpu.VMEM)
    smem = pl.BlockSpec(memory_space=pltpu.SMEM)
    hbm = pl.BlockSpec(memory_space=pl.ANY)
    dma = pltpu.SemaphoreType.DMA
    far, own = pl.pallas_call(
        kernel,
        out_shape=(
            jax.ShapeDtypeStruct((TOK, HEADS * HEAD_DIM), BF16),
            jax.ShapeDtypeStruct((TOK, COLS), F32),
        ),
        in_specs=[smem, smem, vmem, hbm, hbm, hbm, hbm, hbm],
        out_specs=(hbm, hbm),
        scratch_shapes=[
            pltpu.SMEM((16, 2), jnp.int32),
            pltpu.VMEM((2, PAGES_DEV, TOK, HEAD_DIM), BF16),
            pltpu.VMEM((16, 2, 2, TOK, HEAD_DIM), BF16),
            pltpu.VMEM((16, 2, 2, TOK, HEAD_DIM), BF16),
            pltpu.VMEM((4, TOK, COLS), BF16),
            pltpu.VMEM((8, 2, TOK, HEAD_DIM), BF16),
            pltpu.VMEM((4, GROUPS * TOK, 2 * HEAD_DIM), BF16),
            pltpu.VMEM((8, KEYS, 2 * HEAD_DIM), BF16),
            pltpu.VMEM((5, VROWS, KEYS), BF16),
            pltpu.VMEM((8, 1, ROWS), F32),
            pltpu.VMEM((8, VROWS, ROWS), F32),
            pltpu.VMEM((KEYS, ROWS), F32),
            pltpu.VMEM((KEYS, ROWS), F32),
            pltpu.VMEM((1, ROWS), F32),
            pltpu.VMEM((1, ROWS), F32),
            pltpu.VMEM((4, 2, TOK, COLS // 2), BF16),
            pltpu.VMEM((TOK, COLS), F32),
            dma((6,)),
            dma((4,)), dma((4,)),
            dma((8, 2)), dma((8, 2)),
            dma((16,)), dma((16,)),
            dma((4, 2)), dma((4, 2)),
        ],
        compiler_params=pltpu.CompilerParams(
            collective_id=0, has_side_effects=True, vmem_limit_bytes=64000 * 1024),
        name="attend",
    )(page_ids, prefix_pages, page_ids, queries, span_keys, span_values, pool_keys, pool_values)
    def convert(far_ref, own_ref, out_ref):
        head = lax.axis_index("cp") % 4
        out_ref[0] = far_ref[...].astype(F32)
        cols = pl.ds(pl.multiple_of(head * COLS, COLS), COLS)
        out_ref[0, :, cols] = own_ref[...]

    return pl.pallas_call(
        convert,
        out_shape=jax.ShapeDtypeStruct((1, TOK, HEADS * HEAD_DIM), F32),
        grid=(TOK // CONVERT_ROWS,),
        in_specs=[
            pl.BlockSpec((CONVERT_ROWS, HEADS * HEAD_DIM), lambda i: (i, 0)),
            pl.BlockSpec((CONVERT_ROWS, COLS), lambda i: (i, 0)),
        ],
        out_specs=pl.BlockSpec((1, CONVERT_ROWS, HEADS * HEAD_DIM), lambda i: (0, i, 0)),
        name="convert",
    )(far, own)


def solution(mesh):
    in_specs = (
        P("pool", "cp", None),
        P("pool", "cp", None),
        P("pool", "cp", None),
        P("pool", None, None),
        P("pool", None, None),
        P(),
        P(),
    )
    out_specs = P("pool", "cp", None)
    return jax.shard_map(attend, mesh=mesh, in_specs=in_specs, out_specs=out_specs, check_vma=False)
```

```python
import functools

import jax
import jax.numpy as jnp
import numpy as np
from jax import lax
from jax.experimental import pallas as pl
from jax.experimental.pallas import tpu as pltpu
from jax.sharding import PartitionSpec as P

HEAD_DIM = 128
HEADS = 32
KV_HEADS = 4
PAGES_DEV = 24
SLOTS = 32
TOK = 128
GROUPS = HEADS // KV_HEADS
COLS = GROUPS * HEAD_DIM

ROWS = 512
KEYS = 1024
VROWS = 144
NEG = -1e30
SCALE2 = float(HEAD_DIM**-0.5 * np.log2(np.e))
MESH = pl.DeviceIdType.MESH

CHUNK_OWNERS = ((0, 1, 8, 9), (2, 6, 4, 12), (10, 11, 14, 15), (3, 7, 5, 13))
WAVES = ((8, 9, 1, 4, 12), (2, 6), (10, 15), (14, 11), (3, 7))
FAR = (4, 12)
OTHER_X = (9, 11, 15)
BLOCK_XOR = (0, 1, 3, 2)
BF16 = jnp.bfloat16
F32 = jnp.float32
SPAN, LAST = 3, 4
CONVERT_ROWS = 64


def xor(index, offset):
    for bit in range(4):
        if offset >> bit & 1:
            index = index + (1 << bit) * (1 - 2 * ((index // (1 << bit)) % 2))
    return index


def xor_block(index, block):
    low = jnp.where(block == 3, 0, 1)
    high = jnp.where(block == 1, 0, 1)
    index = index + low * (1 - 2 * (index % 2))
    return index + 2 * high * (1 - 2 * ((index // 2) % 2))


def schedule(u):
    chunk = jnp.where(u < 6, u // 3, u - 6)
    block = jnp.where(u < 6, u % 3, 3)
    return chunk, block


def kernel(
    pid, npages, ids_ref, q_ref, sk_ref, sv_ref, pk_ref, pv_ref,
    out_ref, own_ref,
    pgs, pool_v, send_v, kv_v, qbuf, span_v, qaug, kaug, vt, m_ref, acc, s0, s1, x0, x1, obuf, own_v,
    loc_sem, q_send, q_recv, sp_send, sp_recv, pl_send, pl_recv, o_send, o_recv,
):
    me = lax.axis_index("pool")
    ctx = lax.axis_index("cp")
    head = ctx % 4
    my_cols = pl.ds(pl.multiple_of(head * HEAD_DIM, HEAD_DIM), HEAD_DIM)

    def group_cols(index):
        return pl.ds(pl.multiple_of(index * COLS, COLS), COLS)

    local = [
        pltpu.make_async_copy(pk_ref.at[:, :, my_cols], pool_v.at[0], loc_sem.at[0]),
        pltpu.make_async_copy(pv_ref.at[:, :, my_cols], pool_v.at[1], loc_sem.at[1]),
        pltpu.make_async_copy(q_ref.at[0, :, group_cols(head)], qbuf.at[0], loc_sem.at[2]),
        pltpu.make_async_copy(sk_ref.at[0, :, my_cols], span_v.at[0, 0], loc_sem.at[3]),
        pltpu.make_async_copy(sv_ref.at[0, :, my_cols], span_v.at[0, 1], loc_sem.at[4]),
    ]
    for copy in local:
        copy.start()

    barrier = pltpu.get_barrier_semaphore()
    other = xor(ctx, 4)
    later_half = ctx // 4

    def owner(k):
        index = xor(me, k)
        if k in FAR or k - 1 in FAR:
            index = index + later_half * (1 - 2 * (index % 2))
        return index

    def slot_of(k):
        if k in FAR:
            return k + later_half
        return k - later_half if k - 1 in FAR else k

    for wave in WAVES:
        for k in wave:
            pl.semaphore_signal(
                barrier, inc=1, device_id=(owner(k), other if k in OTHER_X else ctx), device_id_type=MESH)
    for k in range(1, 8):
        pl.semaphore_signal(barrier, inc=1, device_id=(me, xor(ctx, k)), device_id_type=MESH)

    base = me * PAGES_DEV

    def scan(r, _):
        live = npages[r]
        first = jnp.int32(0)
        second = jnp.int32(0)
        for s in range(SLOTS):
            page = pid[r, s] - base
            hit = (page >= 0) & (page < PAGES_DEV) & (s < live)
            second = jnp.where(hit, first, second)
            first = jnp.where(hit, page, first)
        pgs[r, 0] = first
        pgs[r, 1] = second
        return 0

    lax.fori_loop(0, 16, scan, 0)
    pl.semaphore_wait(barrier, sum(map(len, WAVES)) + 7)

    q_copies = {}
    for slot in (1, 2, 3):
        mate = xor(ctx, BLOCK_XOR[slot])
        q_copies[slot] = pltpu.make_async_remote_copy(
            src_ref=q_ref.at[0, :, group_cols(mate % 4)], dst_ref=qbuf.at[slot],
            send_sem=q_send.at[slot], recv_sem=q_recv.at[slot],
            device_id=(me, mate), device_id_type=MESH)
    q_copies[1].start()
    q_copies[2].start()

    local[0].wait()
    local[1].wait()

    def pick(k, dst):
        r = owner(k)
        slot = slot_of(k)
        for cap in range(2):
            page = pgs[r, cap]
            dst[slot, 0, cap] = pool_v[0, page]
            dst[slot, 1, cap] = pool_v[1, page]

    pool_copies = {}
    for wave in WAVES:
        for k in wave:
            slot = slot_of(k)
            pool_copies[k] = pltpu.make_async_remote_copy(
                src_ref=send_v.at[slot], dst_ref=kv_v.at[slot],
                send_sem=pl_send.at[slot], recv_sem=pl_recv.at[slot],
                device_id=(owner(k), other if k in OTHER_X else ctx), device_id_type=MESH)

    def passed_on(k, slot):
        return pltpu.make_async_remote_copy(
            src_ref=kv_v.at[slot], dst_ref=kv_v.at[slot],
            send_sem=pl_send.at[2 * k + 1 - slot], recv_sem=pl_recv.at[slot],
            device_id=(me, other), device_id_type=MESH)

    def pass_on():
        for k in FAR:
            pool_copies[k].wait_recv()
            passed_on(k, slot_of(k)).start()

    def send_pages(wave):
        for k in WAVES[wave]:
            pool_copies[k].start()

    for k in WAVES[0]:
        pick(k, send_v)
    pick(0, kv_v)
    send_pages(0)

    span_copies = {}
    for k in range(1, 8):
        mate = xor(ctx, k)
        cols = pl.ds(pl.multiple_of((mate % 4) * HEAD_DIM, HEAD_DIM), HEAD_DIM)
        for which, ref in ((0, sk_ref), (1, sv_ref)):
            span_copies[k, which] = pltpu.make_async_remote_copy(
                src_ref=ref.at[0, :, cols], dst_ref=span_v.at[k, which],
                send_sem=sp_send.at[k, which], recv_sem=sp_recv.at[k, which],
                device_id=(me, mate), device_id_type=MESH)

    for wave in WAVES[1:]:
        for k in wave:
            pick(k, send_v)

    def send_span():
        for k in (1, 3, 2):
            span_copies[k, 0].start()
            span_copies[k, 1].start()

    row_iota = lax.broadcasted_iota(jnp.int32, (TOK, TOK), 0)
    col_iota = lax.broadcasted_iota(jnp.int32, (TOK, TOK), 1)
    eye = jnp.where(row_iota == col_iota, 1.0, 0.0).astype(F32).astype(BF16)
    later = jnp.where(row_iota > col_iota, NEG, 0.0).astype(F32).astype(BF16)
    for slot in range(4):
        for g in range(GROUPS):
            qaug[slot, g * TOK:(g + 1) * TOK, HEAD_DIM:] = eye
    for slot in range(4):
        for k in range(8):
            if BLOCK_XOR[slot] == k:
                mask = later
            else:
                hidden = xor(ctx, k) > xor(ctx, BLOCK_XOR[slot])
                mask = jnp.full((TOK, TOK), jnp.where(hidden, NEG, 0.0), F32).astype(BF16)
            kaug[4 + slot, k * TOK:(k + 1) * TOK, HEAD_DIM:] = mask
    my_ids = ids_ref[pl.ds(me, 1), :]
    slot_iota = lax.broadcasted_iota(jnp.int32, (1, SLOTS), 1)
    my_ids = jnp.where(slot_iota < npages[me], my_ids, -1)
    for j, owners in enumerate(CHUNK_OWNERS):
        for i, k in enumerate(owners):
            low = owner(k) * PAGES_DEV
            held = jnp.where((my_ids >= low) & (my_ids < low + PAGES_DEV), 1.0, 0.0).astype(F32)
            count = jnp.sum(held, axis=1, keepdims=True)
            for cap in range(2):
                bias = jnp.where(count > cap + 0.5, 0.0, NEG)
                at = (2 * i + cap) * TOK
                kaug[j, at:at + TOK, HEAD_DIM:] = jnp.broadcast_to(bias, (TOK, TOK)).astype(BF16)
    vt[:, HEAD_DIM:, :] = jnp.ones((5, VROWS - HEAD_DIM, KEYS), BF16)
    m_ref[...] = jnp.full(m_ref.shape, NEG, F32)
    acc[...] = jnp.zeros(acc.shape, F32)
    s1[...] = jnp.full(s1.shape, NEG, F32)
    x1[...] = jnp.full(x1.shape, NEG, F32)

    def load_block(slot):
        for g in range(GROUPS):
            qaug[slot, g * TOK:(g + 1) * TOK, :HEAD_DIM] = qbuf[slot, :, g * HEAD_DIM:(g + 1) * HEAD_DIM]

    def load_values(chunk, i, values):
        vt[chunk, :HEAD_DIM, i * TOK:(i + 1) * TOK] = values.astype(F32).T.astype(BF16)

    def load_prefix(j):
        for i, k in enumerate(CHUNK_OWNERS[j]):
            if k - 1 in FAR:
                passed_on(k - 1, slot_of(k)).wait_recv()
            elif k and k not in FAR:
                pool_copies[k].wait_recv()
        for i, k in enumerate(CHUNK_OWNERS[j]):
            for cap in range(2):
                at = (2 * i + cap) * TOK
                kaug[j, at:at + TOK, :HEAD_DIM] = kv_v[slot_of(k), 0, cap]
                load_values(j + (j > 2), 2 * i + cap, kv_v[slot_of(k), 1, cap])

    def load_span():
        local[3].wait()
        local[4].wait()
        for k in range(1, 4):
            span_copies[k, 0].wait_recv()
            span_copies[k, 1].wait_recv()

        @pl.when(ctx >= 4)
        def _():
            for k in range(4, 8):
                span_copies[k, 0].wait_recv()
                span_copies[k, 1].wait_recv()

        for k in range(8):
            at = jnp.where(ctx < 4, k % 4, k)
            for slot in range(4):
                kaug[4 + slot, k * TOK:(k + 1) * TOK, :HEAD_DIM] = span_v[at, 0]
            load_values(3, k, span_v[at, 1])

    def scores(chunk, block, half, s_ref, x_ref):
        at = chunk
        if isinstance(chunk, int) and chunk >= SPAN:
            at = 4 + block if chunk == SPAN else 3
        s = lax.dot_general(
            kaug[at], qaug[block, half * ROWS:(half + 1) * ROWS, :],
            (((1,), (1,)), ((), ())), preferred_element_type=F32)
        s_ref[...] = s
        x_ref[...] = jnp.max(s, axis=0, keepdims=True)

    def absorb(chunk, block, half, s_ref, x_ref):
        t = block * 2 + half
        m_old = m_ref[t]
        m_new = jnp.maximum(m_old, x_ref[...])
        alpha = jnp.exp2((m_old - m_new) * SCALE2)
        p = jnp.exp2((s_ref[...] - m_new) * SCALE2).astype(BF16)
        m_ref[t] = m_new
        acc[t] = acc[t] * alpha + jnp.dot(vt[chunk], p, preferred_element_type=F32)

    def body(now, before):
        scores(*now, 0, s0, x0)
        absorb(*before, 1, s1, x1)
        scores(*now, 1, s1, x1)
        absorb(*now, 0, s0, x0)

    def result(block, half, g):
        a = acc.at[block * 2 + half]
        cols = slice(g * TOK, (g + 1) * TOK)
        return (a[:HEAD_DIM, cols] / a[HEAD_DIM:HEAD_DIM + 1, cols]).T

    def out_copy(block, half):
        mate = xor_block(ctx, block)
        cols = pl.ds(pl.multiple_of(head * COLS + half * (COLS // 2), COLS // 2), COLS // 2)
        return pltpu.make_async_remote_copy(
            src_ref=obuf.at[block, half], dst_ref=out_ref.at[:, cols],
            send_sem=o_send.at[block, half], recv_sem=o_recv.at[block, half],
            device_id=(me, mate), device_id_type=MESH)

    def send(block, half):
        for g in range(4):
            obuf[block, half, :, g * HEAD_DIM:(g + 1) * HEAD_DIM] = result(block, half, g).astype(BF16)
        out_copy(block, half).start()

    def keep(half):
        for g in range(4):
            at = (half * 4 + g) * HEAD_DIM
            own_v[:, at:at + HEAD_DIM] = result(0, half, g)

    local[2].wait()
    load_block(0)
    load_prefix(0)
    send_pages(1)
    q_copies[3].start()

    @pl.when(ctx < 4)
    def _():
        for k in (4, 5, 7, 6):
            span_copies[k, 0].start()
            span_copies[k, 1].start()


    def step(u, _):
        for at, wave in ((1, 2), (2, 3), (4, 4)):
            @pl.when(u == at)
            def _():
                send_pages(wave)

        @pl.when(u == 3)
        def _():
            pass_on()

        for at, slot in ((1, 1), (2, 2), (6, 3)):
            @pl.when(u == at)
            def _():
                q_copies[slot].wait_recv()
                load_block(slot)

        @pl.when(u == 3)
        def _():
            load_prefix(1)

        @pl.when(u == 5)
        def _():
            send_span()

        body(schedule(u), schedule(jnp.maximum(u - 1, 0)))
        return 0

    lax.fori_loop(0, 8, step, 0)

    def finish(i, _):
        block = 3 - i

        @pl.when(i == 0)
        def _():
            load_span()

        before = jnp.where(i == 0, 1, 2)
        body((SPAN, block), (before, jnp.minimum(block + 1, 3)))

        @pl.when(i > 0)
        def _():
            send(block + 1, 1)

        @pl.when(i == 0)
        def _():
            load_prefix(3)

        body((LAST, block), (SPAN, block))

        @pl.when(i == 0)
        def _():
            load_prefix(2)

        body((2, block), (LAST, block))

        @pl.when(i < 3)
        def _():
            send(block, 0)

        return 0

    lax.fori_loop(0, 4, finish, 0)
    keep(0)
    absorb(2, 0, 1, s1, x1)
    keep(1)
    own_copy = pltpu.make_async_copy(own_v, own_ref, loc_sem.at[5])
    own_copy.start()

    for slot in (1, 2, 3):
        q_copies[slot].wait_send()
    for wave in WAVES:
        for k in wave:
            pool_copies[k].wait_send()
    for k in FAR:
        passed_on(k, slot_of(k)).wait_send()
    for k in range(1, 4):
        span_copies[k, 0].wait_send()
        span_copies[k, 1].wait_send()

    @pl.when(ctx < 4)
    def _():
        for k in range(4, 8):
            span_copies[k, 0].wait_send()
            span_copies[k, 1].wait_send()

    for block in (3, 2, 1):
        for half in range(2):
            out_copy(block, half).wait()
    own_copy.wait()


def attend(queries, span_keys, span_values, pool_keys, pool_values, page_ids, prefix_pages):
    vmem = pl.BlockSpec(memory_space=pltpu.VMEM)
    smem = pl.BlockSpec(memory_space=pltpu.SMEM)
    hbm = pl.BlockSpec(memory_space=pl.ANY)
    dma = pltpu.SemaphoreType.DMA
    far, own = pl.pallas_call(
        kernel,
        out_shape=(
            jax.ShapeDtypeStruct((TOK, HEADS * HEAD_DIM), BF16),
            jax.ShapeDtypeStruct((TOK, COLS), F32),
        ),
        in_specs=[smem, smem, vmem, hbm, hbm, hbm, hbm, hbm],
        out_specs=(hbm, hbm),
        scratch_shapes=[
            pltpu.SMEM((16, 2), jnp.int32),
            pltpu.VMEM((2, PAGES_DEV, TOK, HEAD_DIM), BF16),
            pltpu.VMEM((16, 2, 2, TOK, HEAD_DIM), BF16),
            pltpu.VMEM((16, 2, 2, TOK, HEAD_DIM), BF16),
            pltpu.VMEM((4, TOK, COLS), BF16),
            pltpu.VMEM((8, 2, TOK, HEAD_DIM), BF16),
            pltpu.VMEM((4, GROUPS * TOK, 2 * HEAD_DIM), BF16),
            pltpu.VMEM((8, KEYS, 2 * HEAD_DIM), BF16),
            pltpu.VMEM((5, VROWS, KEYS), BF16),
            pltpu.VMEM((8, 1, ROWS), F32),
            pltpu.VMEM((8, VROWS, ROWS), F32),
            pltpu.VMEM((KEYS, ROWS), F32),
            pltpu.VMEM((KEYS, ROWS), F32),
            pltpu.VMEM((1, ROWS), F32),
            pltpu.VMEM((1, ROWS), F32),
            pltpu.VMEM((4, 2, TOK, COLS // 2), BF16),
            pltpu.VMEM((TOK, COLS), F32),
            dma((6,)),
            dma((4,)), dma((4,)),
            dma((8, 2)), dma((8, 2)),
            dma((16,)), dma((16,)),
            dma((4, 2)), dma((4, 2)),
        ],
        compiler_params=pltpu.CompilerParams(
            collective_id=0, has_side_effects=True, vmem_limit_bytes=64000 * 1024),
        name="attend",
    )(page_ids, prefix_pages, page_ids, queries, span_keys, span_values, pool_keys, pool_values)
    def convert(far_ref, own_ref, out_ref):
        head = lax.axis_index("cp") % 4
        out_ref[0] = far_ref[...].astype(F32)
        cols = pl.ds(pl.multiple_of(head * COLS, COLS), COLS)
        out_ref[0, :, cols] = own_ref[...]

    return pl.pallas_call(
        convert,
        out_shape=jax.ShapeDtypeStruct((1, TOK, HEADS * HEAD_DIM), F32),
        grid=(TOK // CONVERT_ROWS,),
        in_specs=[
            pl.BlockSpec((CONVERT_ROWS, HEADS * HEAD_DIM), lambda i: (i, 0)),
            pl.BlockSpec((CONVERT_ROWS, COLS), lambda i: (i, 0)),
        ],
        out_specs=pl.BlockSpec((1, CONVERT_ROWS, HEADS * HEAD_DIM), lambda i: (0, i, 0)),
        name="convert",
    )(far, own)


def solution(mesh):
    in_specs = (
        P("pool", "cp", None),
        P("pool", "cp", None),
        P("pool", "cp", None),
        P("pool", None, None),
        P("pool", None, None),
        P(),
        P(),
    )
    out_specs = P("pool", "cp", None)
    return jax.shard_map(attend, mesh=mesh, in_specs=in_specs, out_specs=out_specs, check_vma=False)
```

```python
import functools

import jax
import jax.numpy as jnp
import numpy as np
from jax import lax
from jax.experimental import pallas as pl
from jax.experimental.pallas import tpu as pltpu
from jax.sharding import PartitionSpec as P

HEAD_DIM = 128
HEADS = 32
KV_HEADS = 4
PAGES_DEV = 24
SLOTS = 32
TOK = 128
GROUPS = HEADS // KV_HEADS
COLS = GROUPS * HEAD_DIM

ROWS = 512
KEYS = 1024
VROWS = 144
NEG = -1e30
SCALE2 = float(HEAD_DIM**-0.5 * np.log2(np.e))
MESH = pl.DeviceIdType.MESH

CHUNK_OWNERS = ((0, 1, 8, 9), (2, 6, 4, 12), (10, 11, 14, 15), (3, 7, 5, 13))
WAVES = ((8, 9, 1, 4, 12), (2, 6), (10, 15), (14, 11), (3, 7))
FAR = (4, 12)
OTHER_X = (9, 11, 15)
BLOCK_XOR = (0, 1, 3, 2)
BF16 = jnp.bfloat16
F32 = jnp.float32
SPAN, LAST = 3, 4
CONVERT_ROWS = 64


def xor(index, offset):
    for bit in range(4):
        if offset >> bit & 1:
            index = index + (1 << bit) * (1 - 2 * ((index // (1 << bit)) % 2))
    return index


def xor_block(index, block):
    low = jnp.where(block == 3, 0, 1)
    high = jnp.where(block == 1, 0, 1)
    index = index + low * (1 - 2 * (index % 2))
    return index + 2 * high * (1 - 2 * ((index // 2) % 2))


def schedule(u):
    chunk = jnp.where(u < 6, u // 3, u - 6)
    block = jnp.where(u < 6, u % 3, 3)
    return chunk, block


def kernel(
    pid, npages, ids_ref, q_ref, sk_ref, sv_ref, pk_ref, pv_ref,
    out_ref, own_ref,
    pgs, pool_v, send_v, kv_v, qbuf, span_v, qaug, kaug, vt, m_ref, acc, s0, s1, x0, x1, obuf, own_v,
    loc_sem, q_send, q_recv, sp_send, sp_recv, pl_send, pl_recv, o_send, o_recv,
):
    me = lax.axis_index("pool")
    ctx = lax.axis_index("cp")
    head = ctx % 4
    my_cols = pl.ds(pl.multiple_of(head * HEAD_DIM, HEAD_DIM), HEAD_DIM)

    def group_cols(index):
        return pl.ds(pl.multiple_of(index * COLS, COLS), COLS)

    local = [
        pltpu.make_async_copy(pk_ref.at[:, :, my_cols], pool_v.at[0], loc_sem.at[0]),
        pltpu.make_async_copy(pv_ref.at[:, :, my_cols], pool_v.at[1], loc_sem.at[1]),
        pltpu.make_async_copy(q_ref.at[0, :, group_cols(head)], qbuf.at[0], loc_sem.at[2]),
        pltpu.make_async_copy(sk_ref.at[0, :, my_cols], span_v.at[0, 0], loc_sem.at[3]),
        pltpu.make_async_copy(sv_ref.at[0, :, my_cols], span_v.at[0, 1], loc_sem.at[4]),
    ]
    for copy in local:
        copy.start()

    barrier = pltpu.get_barrier_semaphore()
    other = xor(ctx, 4)
    later_half = ctx // 4

    def owner(k):
        index = xor(me, k)
        if k in FAR or k - 1 in FAR:
            index = index + later_half * (1 - 2 * (index % 2))
        return index

    def slot_of(k):
        if k in FAR:
            return k + later_half
        return k - later_half if k - 1 in FAR else k

    for wave in WAVES:
        for k in wave:
            pl.semaphore_signal(
                barrier, inc=1, device_id=(owner(k), other if k in OTHER_X else ctx), device_id_type=MESH)
    for k in range(1, 8):
        pl.semaphore_signal(barrier, inc=1, device_id=(me, xor(ctx, k)), device_id_type=MESH)

    base = me * PAGES_DEV

    def scan(r, _):
        live = npages[r]
        first = jnp.int32(0)
        second = jnp.int32(0)
        for s in range(SLOTS):
            page = pid[r, s] - base
            hit = (page >= 0) & (page < PAGES_DEV) & (s < live)
            second = jnp.where(hit, first, second)
            first = jnp.where(hit, page, first)
        pgs[r, 0] = first
        pgs[r, 1] = second
        return 0

    lax.fori_loop(0, 16, scan, 0)
    local[0].wait()
    local[1].wait()

    def pick(k, dst):
        r = owner(k)
        slot = slot_of(k)
        for cap in range(2):
            page = pgs[r, cap]
            dst[slot, 0, cap] = pool_v[0, page]
            dst[slot, 1, cap] = pool_v[1, page]

    for k in WAVES[0]:
        pick(k, send_v)
    pl.semaphore_wait(barrier, sum(map(len, WAVES)) + 7)

    q_copies = {}
    for slot in (1, 2, 3):
        mate = xor(ctx, BLOCK_XOR[slot])
        q_copies[slot] = pltpu.make_async_remote_copy(
            src_ref=q_ref.at[0, :, group_cols(mate % 4)], dst_ref=qbuf.at[slot],
            send_sem=q_send.at[slot], recv_sem=q_recv.at[slot],
            device_id=(me, mate), device_id_type=MESH)
    q_copies[1].start()
    q_copies[2].start()

    pool_copies = {}
    for wave in WAVES:
        for k in wave:
            slot = slot_of(k)
            pool_copies[k] = pltpu.make_async_remote_copy(
                src_ref=send_v.at[slot], dst_ref=kv_v.at[slot],
                send_sem=pl_send.at[slot], recv_sem=pl_recv.at[slot],
                device_id=(owner(k), other if k in OTHER_X else ctx), device_id_type=MESH)

    def passed_on(k, slot):
        return pltpu.make_async_remote_copy(
            src_ref=kv_v.at[slot], dst_ref=kv_v.at[slot],
            send_sem=pl_send.at[2 * k + 1 - slot], recv_sem=pl_recv.at[slot],
            device_id=(me, other), device_id_type=MESH)

    def pass_on():
        for k in FAR:
            pool_copies[k].wait_recv()
            passed_on(k, slot_of(k)).start()

    def send_pages(wave):
        for k in WAVES[wave]:
            pool_copies[k].start()

    send_pages(0)
    pick(0, kv_v)

    span_copies = {}
    for k in range(1, 8):
        mate = xor(ctx, k)
        cols = pl.ds(pl.multiple_of((mate % 4) * HEAD_DIM, HEAD_DIM), HEAD_DIM)
        for which, ref in ((0, sk_ref), (1, sv_ref)):
            span_copies[k, which] = pltpu.make_async_remote_copy(
                src_ref=ref.at[0, :, cols], dst_ref=span_v.at[k, which],
                send_sem=sp_send.at[k, which], recv_sem=sp_recv.at[k, which],
                device_id=(me, mate), device_id_type=MESH)

    for wave in WAVES[1:]:
        for k in wave:
            pick(k, send_v)

    def send_span():
        for k in (1, 3, 2):
            span_copies[k, 0].start()
            span_copies[k, 1].start()

    row_iota = lax.broadcasted_iota(jnp.int32, (TOK, TOK), 0)
    col_iota = lax.broadcasted_iota(jnp.int32, (TOK, TOK), 1)
    eye = jnp.where(row_iota == col_iota, 1.0, 0.0).astype(F32).astype(BF16)
    later = jnp.where(row_iota > col_iota, NEG, 0.0).astype(F32).astype(BF16)
    for slot in range(4):
        for g in range(GROUPS):
            qaug[slot, g * TOK:(g + 1) * TOK, HEAD_DIM:] = eye
    for slot in range(4):
        for k in range(8):
            if BLOCK_XOR[slot] == k:
                mask = later
            else:
                hidden = xor(ctx, k) > xor(ctx, BLOCK_XOR[slot])
                mask = jnp.full((TOK, TOK), jnp.where(hidden, NEG, 0.0), F32).astype(BF16)
            kaug[4 + slot, k * TOK:(k + 1) * TOK, HEAD_DIM:] = mask
    my_ids = ids_ref[pl.ds(me, 1), :]
    slot_iota = lax.broadcasted_iota(jnp.int32, (1, SLOTS), 1)
    my_ids = jnp.where(slot_iota < npages[me], my_ids, -1)
    for j, owners in enumerate(CHUNK_OWNERS):
        for i, k in enumerate(owners):
            low = owner(k) * PAGES_DEV
            held = jnp.where((my_ids >= low) & (my_ids < low + PAGES_DEV), 1.0, 0.0).astype(F32)
            count = jnp.sum(held, axis=1, keepdims=True)
            for cap in range(2):
                bias = jnp.where(count > cap + 0.5, 0.0, NEG)
                at = (2 * i + cap) * TOK
                kaug[j, at:at + TOK, HEAD_DIM:] = jnp.broadcast_to(bias, (TOK, TOK)).astype(BF16)
    vt[:, HEAD_DIM:, :] = jnp.ones((5, VROWS - HEAD_DIM, KEYS), BF16)
    m_ref[...] = jnp.full(m_ref.shape, NEG, F32)
    acc[...] = jnp.zeros(acc.shape, F32)
    s1[...] = jnp.full(s1.shape, NEG, F32)
    x1[...] = jnp.full(x1.shape, NEG, F32)

    def load_block(slot):
        for g in range(GROUPS):
            qaug[slot, g * TOK:(g + 1) * TOK, :HEAD_DIM] = qbuf[slot, :, g * HEAD_DIM:(g + 1) * HEAD_DIM]

    def load_values(chunk, i, values):
        vt[chunk, :HEAD_DIM, i * TOK:(i + 1) * TOK] = values.astype(F32).T.astype(BF16)

    def load_prefix(j):
        for i, k in enumerate(CHUNK_OWNERS[j]):
            if k - 1 in FAR:
                passed_on(k - 1, slot_of(k)).wait_recv()
            elif k and k not in FAR:
                pool_copies[k].wait_recv()
        for i, k in enumerate(CHUNK_OWNERS[j]):
            for cap in range(2):
                at = (2 * i + cap) * TOK
                kaug[j, at:at + TOK, :HEAD_DIM] = kv_v[slot_of(k), 0, cap]
                load_values(j + (j > 2), 2 * i + cap, kv_v[slot_of(k), 1, cap])

    def load_span():
        local[3].wait()
        local[4].wait()
        for k in range(1, 4):
            span_copies[k, 0].wait_recv()
            span_copies[k, 1].wait_recv()

        @pl.when(ctx >= 4)
        def _():
            for k in range(4, 8):
                span_copies[k, 0].wait_recv()
                span_copies[k, 1].wait_recv()

        for k in range(8):
            at = jnp.where(ctx < 4, k % 4, k)
            for slot in range(4):
                kaug[4 + slot, k * TOK:(k + 1) * TOK, :HEAD_DIM] = span_v[at, 0]
            load_values(3, k, span_v[at, 1])

    def scores(chunk, block, half, s_ref, x_ref):
        at = chunk
        if isinstance(chunk, int) and chunk >= SPAN:
            at = 4 + block if chunk == SPAN else 3
        s = lax.dot_general(
            kaug[at], qaug[block, half * ROWS:(half + 1) * ROWS, :],
            (((1,), (1,)), ((), ())), preferred_element_type=F32)
        s_ref[...] = s
        x_ref[...] = jnp.max(s, axis=0, keepdims=True)

    def absorb(chunk, block, half, s_ref, x_ref):
        t = block * 2 + half
        m_old = m_ref[t]
        m_new = jnp.maximum(m_old, x_ref[...])
        alpha = jnp.exp2((m_old - m_new) * SCALE2)
        p = jnp.exp2((s_ref[...] - m_new) * SCALE2).astype(BF16)
        m_ref[t] = m_new
        acc[t] = acc[t] * alpha + jnp.dot(vt[chunk], p, preferred_element_type=F32)

    def body(now, before):
        scores(*now, 0, s0, x0)
        absorb(*before, 1, s1, x1)
        scores(*now, 1, s1, x1)
        absorb(*now, 0, s0, x0)

    def result(block, half, g):
        a = acc.at[block * 2 + half]
        cols = slice(g * TOK, (g + 1) * TOK)
        return (a[:HEAD_DIM, cols] / a[HEAD_DIM:HEAD_DIM + 1, cols]).T

    def out_copy(block, half):
        mate = xor_block(ctx, block)
        cols = pl.ds(pl.multiple_of(head * COLS + half * (COLS // 2), COLS // 2), COLS // 2)
        return pltpu.make_async_remote_copy(
            src_ref=obuf.at[block, half], dst_ref=out_ref.at[:, cols],
            send_sem=o_send.at[block, half], recv_sem=o_recv.at[block, half],
            device_id=(me, mate), device_id_type=MESH)

    def send(block, half):
        for g in range(4):
            obuf[block, half, :, g * HEAD_DIM:(g + 1) * HEAD_DIM] = result(block, half, g).astype(BF16)
        out_copy(block, half).start()

    def keep(half):
        for g in range(4):
            at = (half * 4 + g) * HEAD_DIM
            own_v[:, at:at + HEAD_DIM] = result(0, half, g)

    local[2].wait()
    load_block(0)
    load_prefix(0)
    send_pages(1)
    q_copies[3].start()

    @pl.when(ctx < 4)
    def _():
        for k in (4, 5, 7, 6):
            span_copies[k, 0].start()
            span_copies[k, 1].start()


    def step(u, _):
        for at, wave in ((1, 2), (2, 3), (4, 4)):
            @pl.when(u == at)
            def _():
                send_pages(wave)

        @pl.when(u == 3)
        def _():
            pass_on()

        for at, slot in ((1, 1), (2, 2), (6, 3)):
            @pl.when(u == at)
            def _():
                q_copies[slot].wait_recv()
                load_block(slot)

        @pl.when(u == 3)
        def _():
            load_prefix(1)

        @pl.when(u == 5)
        def _():
            send_span()

        body(schedule(u), schedule(jnp.maximum(u - 1, 0)))
        return 0

    lax.fori_loop(0, 8, step, 0)

    def finish(i, _):
        block = 3 - i

        @pl.when(i == 0)
        def _():
            load_span()

        before = jnp.where(i == 0, 1, LAST)
        body((SPAN, block), (before, jnp.minimum(block + 1, 3)))

        @pl.when(i > 0)
        def _():
            send(block + 1, 1)

        @pl.when(i == 0)
        def _():
            load_prefix(2)

        body((2, block), (SPAN, block))

        @pl.when(i == 0)
        def _():
            load_prefix(3)

        body((LAST, block), (2, block))

        @pl.when(i < 3)
        def _():
            send(block, 0)

        return 0

    lax.fori_loop(0, 4, finish, 0)
    keep(0)
    absorb(LAST, 0, 1, s1, x1)
    keep(1)
    own_copy = pltpu.make_async_copy(own_v, own_ref, loc_sem.at[5])
    own_copy.start()

    for slot in (1, 2, 3):
        q_copies[slot].wait_send()
    for wave in WAVES:
        for k in wave:
            pool_copies[k].wait_send()
    for k in FAR:
        passed_on(k, slot_of(k)).wait_send()
    for k in range(1, 4):
        span_copies[k, 0].wait_send()
        span_copies[k, 1].wait_send()

    @pl.when(ctx < 4)
    def _():
        for k in range(4, 8):
            span_copies[k, 0].wait_send()
            span_copies[k, 1].wait_send()

    for block in (3, 2, 1):
        for half in range(2):
            out_copy(block, half).wait()
    own_copy.wait()


def attend(queries, span_keys, span_values, pool_keys, pool_values, page_ids, prefix_pages):
    vmem = pl.BlockSpec(memory_space=pltpu.VMEM)
    smem = pl.BlockSpec(memory_space=pltpu.SMEM)
    hbm = pl.BlockSpec(memory_space=pl.ANY)
    dma = pltpu.SemaphoreType.DMA
    far, own = pl.pallas_call(
        kernel,
        out_shape=(
            jax.ShapeDtypeStruct((TOK, HEADS * HEAD_DIM), BF16),
            jax.ShapeDtypeStruct((TOK, COLS), F32),
        ),
        in_specs=[smem, smem, vmem, hbm, hbm, hbm, hbm, hbm],
        out_specs=(hbm, hbm),
        scratch_shapes=[
            pltpu.SMEM((16, 2), jnp.int32),
            pltpu.VMEM((2, PAGES_DEV, TOK, HEAD_DIM), BF16),
            pltpu.VMEM((16, 2, 2, TOK, HEAD_DIM), BF16),
            pltpu.VMEM((16, 2, 2, TOK, HEAD_DIM), BF16),
            pltpu.VMEM((4, TOK, COLS), BF16),
            pltpu.VMEM((8, 2, TOK, HEAD_DIM), BF16),
            pltpu.VMEM((4, GROUPS * TOK, 2 * HEAD_DIM), BF16),
            pltpu.VMEM((8, KEYS, 2 * HEAD_DIM), BF16),
            pltpu.VMEM((5, VROWS, KEYS), BF16),
            pltpu.VMEM((8, 1, ROWS), F32),
            pltpu.VMEM((8, VROWS, ROWS), F32),
            pltpu.VMEM((KEYS, ROWS), F32),
            pltpu.VMEM((KEYS, ROWS), F32),
            pltpu.VMEM((1, ROWS), F32),
            pltpu.VMEM((1, ROWS), F32),
            pltpu.VMEM((4, 2, TOK, COLS // 2), BF16),
            pltpu.VMEM((TOK, COLS), F32),
            dma((6,)),
            dma((4,)), dma((4,)),
            dma((8, 2)), dma((8, 2)),
            dma((16,)), dma((16,)),
            dma((4, 2)), dma((4, 2)),
        ],
        compiler_params=pltpu.CompilerParams(
            collective_id=0, has_side_effects=True, vmem_limit_bytes=64000 * 1024),
        name="attend",
    )(page_ids, prefix_pages, page_ids, queries, span_keys, span_values, pool_keys, pool_values)
    def convert(far_ref, own_ref, out_ref):
        head = lax.axis_index("cp") % 4
        out_ref[0] = far_ref[...].astype(F32)
        cols = pl.ds(pl.multiple_of(head * COLS, COLS), COLS)
        out_ref[0, :, cols] = own_ref[...]

    return pl.pallas_call(
        convert,
        out_shape=jax.ShapeDtypeStruct((1, TOK, HEADS * HEAD_DIM), F32),
        grid=(TOK // CONVERT_ROWS,),
        in_specs=[
            pl.BlockSpec((CONVERT_ROWS, HEADS * HEAD_DIM), lambda i: (i, 0)),
            pl.BlockSpec((CONVERT_ROWS, COLS), lambda i: (i, 0)),
        ],
        out_specs=pl.BlockSpec((1, CONVERT_ROWS, HEADS * HEAD_DIM), lambda i: (0, i, 0)),
        name="convert",
    )(far, own)


def solution(mesh):
    in_specs = (
        P("pool", "cp", None),
        P("pool", "cp", None),
        P("pool", "cp", None),
        P("pool", None, None),
        P("pool", None, None),
        P(),
        P(),
    )
    out_specs = P("pool", "cp", None)
    return jax.shard_map(attend, mesh=mesh, in_specs=in_specs, out_specs=out_specs, check_vma=False)
```
